256 devices in a mesh: dp: 16 (over z_hi, y, core), tensor: 16 (over x, z_lo).
Axes of the slice: x: 4, y: 4, z: 8 (z_hi: 2, z_lo: 4; z = z_hi * 4 + z_lo), core: 2. Of those that a mesh axis runs over, the one named last changes fastest.
Arguments:
- tokens: bfloat16 [4096, 8192], P('dp'), may hold values from -6 to 6
- gate_weight: bfloat16 [8192, 14336], P('dp', 'tensor'), may hold values from -0.0625 to 0.0625
- up_weight: bfloat16 [8192, 14336], P('dp', 'tensor'), may hold values from -0.0625 to 0.0625
- test_matrix: bfloat16 [14336, 512], P('tensor'), may hold values from -6 to 6
- sketch_old: float32 [14336, 512], P('tensor', 'dp'), may hold values from -6 to 6
Outputs:
- sketch_new: float32 [14336, 512], P('tensor', 'dp')
The draws below stay inside these ranges and needn't reach their ends.
All inputs are finite; a program needn't handle non-finite values.
Results may differ from the reference program's by a relative error of at most 0.02.
Values may be sent and summed in bfloat16 or wider, within the bound.
No kernel may reach another device: no remote copies, remote signals or barrier semaphores. Data moves between devices by JAX's collectives and lax.ppermute only.
A program may use at most 128 MiB of HBM per device.

```python
import jax
import jax.numpy as jnp
from jax import lax

D = 8192
FF = 14336
R = 512
TOKENS = 4096
DBLK = 512


def levels(key, extent, pieces, smallest, top_value):
    level = 1.0
    for dim, shards_of in pieces:
        steps = jax.random.uniform(jax.random.fold_in(jax.random.fold_in(key, 6), dim), (shards_of,), jnp.float32, smallest / len(pieces), top_value / len(pieces))
        level = level * jnp.repeat(jnp.exp(steps), extent[dim] // shards_of).reshape((-1,) + (1,) * (len(extent) - 1 - dim))
    return level


def scatter_about(own_key, shape, spread, reach, pieces=(), kind=jnp.bfloat16):
    loudness = levels(own_key, shape, pieces, -0.22, 0.18) if pieces else 1.0
    result = jax.random.normal(own_key, shape, jnp.float32) * spread * loudness
    return jnp.minimum(jnp.maximum(result, -reach), reach).astype(kind)


def setup_inputs(seed: int = 0) -> dict:
    arg_keys = jax.random.split(jax.random.key(seed), 6)
    return {
        "tokens": scatter_about(arg_keys[0], (TOKENS, D), 1.0, 6.0, ((0, 16),)),
        "gate_weight": scatter_about(arg_keys[1], (D, FF), D ** -0.5, 0.0625, ((0, 16), (1, 16))),
        "up_weight": scatter_about(arg_keys[2], (D, FF), D ** -0.5, 0.0625, ((0, 16), (1, 16))),
        "test_matrix": scatter_about(arg_keys[3], (FF, R), 1.0, 6.0, ((0, 16),)),
        "sketch_old": scatter_about(arg_keys[4], (FF, R), 1.0, 6.0, ((0, 16), (1, 16)), jnp.float32),
    }


def block_sum(tokens, weight):
    total = jnp.zeros((tokens.shape[0], weight.shape[1]), jnp.float32)
    for block in range(D // DBLK):
        first = block * DBLK
        term = jnp.dot(tokens[:, first:first + DBLK], weight[first:first + DBLK], preferred_element_type=jnp.float32)
        term = lax.optimization_barrier(term.astype(jnp.bfloat16))
        total = total + term.astype(jnp.float32)
    return total


def reference(tokens, gate_weight, up_weight, test_matrix, sketch_old):
    gate = block_sum(tokens, gate_weight)
    up = block_sum(tokens, up_weight)
    hidden = (jax.nn.silu(gate) * up).astype(jnp.bfloat16)
    projected = jnp.dot(hidden, test_matrix, preferred_element_type=jnp.float32).astype(jnp.bfloat16)
    update = lax.dot_general(hidden, projected, (((0,), (0,)), ((), ())), preferred_element_type=jnp.float32)
    return sketch_old + update / TOKENS
```

```python
import jax
import jax.numpy as jnp
from jax import lax
from jax.experimental import pallas as pl
from jax.experimental.pallas import tpu as pltpu
from jax.sharding import Mesh, PartitionSpec as P


AXES = ("zh", "y", "c", "x", "zl")
SIZES = (2, 4, 2, 4, 4)
BF = jnp.bfloat16
F32 = jnp.float32


def shift(value, **moves):
    pairs = []
    total = 1
    for size in SIZES:
        total *= size
    for src in range(total):
        rest = src
        coords = []
        for size in reversed(SIZES):
            coords.append(rest % size)
            rest //= size
        coords = coords[::-1]
        dst = 0
        for name, size, at in zip(AXES, SIZES, coords):
            dst = dst * size + (at + moves.get(name, 0)) % size
        pairs.append((src, dst))
    return lax.ppermute(value, AXES, pairs)


def pick_columns(tokens, blocks, width):
    rows = tokens.shape[0]
    count = blocks.shape[0]

    def body(idx_ref, src_ref, dst_ref):
        dst_ref[0] = src_ref[...]

    return pl.pallas_call(
        body,
        grid_spec=pltpu.PrefetchScalarGridSpec(
            num_scalar_prefetch=1,
            grid=(count,),
            in_specs=[pl.BlockSpec((rows, width), lambda i, idx: (0, idx[i]))],
            out_specs=pl.BlockSpec((1, rows, width), lambda i, idx: (i, 0, 0)),
        ),
        out_shape=jax.ShapeDtypeStruct((count, rows, width), tokens.dtype),
        cost_estimate=pl.CostEstimate(
            flops=0, bytes_accessed=4 * count * rows * width, transcendentals=0
        ),
    )(blocks, tokens)


def local(tokens, gate_weight, up_weight, test_matrix, sketch_old):
    zh, y, c, x = (lax.axis_index(name) for name in ("zh", "y", "c", "x"))
    rows = tokens.shape[0]
    blk, width = gate_weight.shape
    steps = (0, 3, 1, 2)

    g = {0: gate_weight}
    u = {0: up_weight}
    g[3] = shift(gate_weight, y=1)
    g[1] = shift(gate_weight, y=-1)
    u[3] = shift(up_weight, y=1)
    u[1] = shift(up_weight, y=-1)
    g[2] = shift(g[3], y=1)
    u[2] = shift(u[1], y=-1)

    far = ((1 - zh) * 4 + x) * 2
    z_send = pick_columns(tokens, jnp.stack([far + c, far + 1 - c]).astype(jnp.int32), blk)
    near = [(zh * 4 + (y + s) % 4) * 2 for s in steps]
    c_send = pick_columns(tokens, jnp.stack([n + 1 - c for n in near]).astype(jnp.int32), blk)
    own = pick_columns(tokens, jnp.stack([n + c for n in near]).astype(jnp.int32), blk)
    z_got = shift(z_send, zh=1)
    c_got = shift(c_send, c=1)
    z_cross = shift(z_got[1], c=1)
    piece = jnp.stack([z_got[0], z_cross])
    pieces = jnp.stack(
        [piece, shift(piece, x=-1), shift(piece, x=2), shift(piece, x=1)]
    )

    gate = None
    up = None
    for i, s in enumerate(steps):
        other = lax.dynamic_index_in_dim(pieces, (y + s - x) % 4, 0, keepdims=False)
        lhs = jnp.concatenate([own[i], other[0], c_got[i], other[1]], axis=0)
        gp = jnp.dot(lhs, g[s], preferred_element_type=F32)
        up_p = jnp.dot(lhs, u[s], preferred_element_type=F32)
        gate = gp if gate is None else gate + gp
        up = up_p if up is None else up + up_p

    def finish(part):
        got = shift(part[2 * rows :].astype(BF), c=1)
        both = part[: 2 * rows] + got.astype(F32)
        send = both[rows:].astype(BF)
        cut = rows // 4
        back = jnp.concatenate(
            [shift(send[k * cut : (k + 1) * cut], zh=1) for k in range(4)], axis=0
        )
        return both[:rows] + back.astype(F32)

    gate = finish(gate)
    up = finish(up)
    hidden = (jax.nn.silu(gate) * up).astype(BF)

    rank = test_matrix.shape[1]
    part = jnp.dot(hidden, test_matrix, preferred_element_type=F32).astype(BF)
    part = lax.all_to_all(part.reshape(16, rows // 16, rank), ("x", "zl"), 0, 0, tiled=True)
    mine = jnp.sum(part.astype(F32), axis=0).astype(BF)
    spread = jnp.broadcast_to(mine[None], (16,) + mine.shape)
    projected = lax.all_to_all(spread, ("x", "zl"), 0, 0, tiled=True).reshape(rows, rank)

    update = lax.dot_general(
        projected, hidden, (((0,), (0,)), ((), ())), preferred_element_type=F32
    )
    update = update.astype(BF).reshape(16, rank // 16, width)
    update = lax.all_to_all(update, ("zh", "y", "c"), 0, 0, tiled=True)
    summed = jnp.sum(update.astype(F32), axis=0)
    return sketch_old + summed.T / (rows * 16)


def solution(mesh):
    fine = Mesh(mesh.devices.reshape(SIZES), AXES)
    dp = ("zh", "y", "c")
    tensor = ("x", "zl")
    in_specs = (P(dp, None), P(dp, tensor), P(dp, tensor), P(tensor, None), P(tensor, dp))
    return jax.shard_map(
        local, mesh=fine, in_specs=in_specs, out_specs=P(tensor, dp), check_vma=False
    )
```

```python
import jax
import jax.numpy as jnp
from jax import lax
from jax.experimental import pallas as pl
from jax.experimental.pallas import tpu as pltpu
from jax.sharding import Mesh, PartitionSpec as P


AXES = ("zh", "y", "c", "x", "zl")
SIZES = (2, 4, 2, 4, 4)
BF = jnp.bfloat16
F32 = jnp.float32


def shift(value, **moves):
    pairs = []
    total = 1
    for size in SIZES:
        total *= size
    for src in range(total):
        rest = src
        coords = []
        for size in reversed(SIZES):
            coords.append(rest % size)
            rest //= size
        coords = coords[::-1]
        dst = 0
        for name, size, at in zip(AXES, SIZES, coords):
            dst = dst * size + (at + moves.get(name, 0)) % size
        pairs.append((src, dst))
    return lax.ppermute(value, AXES, pairs)


def pick_columns(tokens, blocks, width):
    rows = tokens.shape[0]
    count = blocks.shape[0]

    def body(idx_ref, src_ref, dst_ref):
        dst_ref[0] = src_ref[...]

    return pl.pallas_call(
        body,
        grid_spec=pltpu.PrefetchScalarGridSpec(
            num_scalar_prefetch=1,
            grid=(count,),
            in_specs=[pl.BlockSpec((rows, width), lambda i, idx: (0, idx[i]))],
            out_specs=pl.BlockSpec((1, rows, width), lambda i, idx: (i, 0, 0)),
        ),
        out_shape=jax.ShapeDtypeStruct((count, rows, width), tokens.dtype),
        cost_estimate=pl.CostEstimate(
            flops=0, bytes_accessed=4 * count * rows * width, transcendentals=0
        ),
    )(blocks, tokens)


def after(values, *earlier):
    out = lax.optimization_barrier(tuple(values) + earlier)
    return out[: len(values)]


def named(value, **moves):
    return shift(value, **moves)


def window(tokens, gate_weight, up_weight, test_matrix, sketch_old):
    zh, y, c, x = (lax.axis_index(name) for name in ("zh", "y", "c", "x"))
    rows = tokens.shape[0]
    blk, width = gate_weight.shape
    rank = test_matrix.shape[1]
    cut = blk // 2

    far = ((1 - zh) * 4 + x) * 2
    cross = pick_columns(tokens, jnp.stack([far + 1 - c]).astype(jnp.int32), blk)
    keep = pick_columns(tokens, jnp.stack([far + c]).astype(jnp.int32), blk)
    (gate_in,) = after((gate_weight,), cross, keep)
    cross = named(named(cross, zh=1), c=1)
    keep = named(keep, zh=1)

    g_before = named(gate_in, y=1)
    g_after = named(gate_in, y=-1)
    g_low, g_high, up_in = after((g_before[:cut], g_after[cut:], up_weight))
    g = (gate_weight, g_after, named(g_low, y=1), named(g_high, y=-1), g_before)

    near = [(zh * 4 + (y + s) % 4) * 2 for s in range(4)]
    c_send = pick_columns(tokens, jnp.stack([n + 1 - c for n in near]).astype(jnp.int32), blk)
    near_own = pick_columns(tokens, jnp.stack([n + c for n in near]).astype(jnp.int32), blk)
    near_rows = [near_own, named(c_send, c=1)]

    far_rows = []
    for piece in (cross, keep):
        got = [piece, named(piece, x=-1), named(piece, x=2), named(piece, x=1)]
        got = after(got, near_own)
        slots = jnp.zeros((4, rows, blk), BF)
        for e in range(4):
            slots = lax.dynamic_update_slice_in_dim(slots, got[e], (x + e - y) % 4, 0)
        far_rows.append(slots)
    far_rows = far_rows[::-1]

    u_before = named(up_in, y=1)
    u_after = named(up_in, y=-1)

    def times(lhs, w):
        weight, after, low, high, before = w
        return (
            jnp.dot(lhs[0], weight, preferred_element_type=F32)
            + jnp.dot(lhs[1], after, preferred_element_type=F32)
            + jnp.dot(lhs[3], before, preferred_element_type=F32)
            + jnp.dot(lhs[2, :, :cut], low, preferred_element_type=F32)
            + jnp.dot(lhs[2, :, cut:], high, preferred_element_type=F32)
        )

    def over_cores(lhs, w):
        got = shift(times(lhs[1], w).astype(BF), c=1)
        return times(lhs[0], w) + got.astype(F32)

    gate_send = over_cores(far_rows, g).astype(BF)
    gate_back = named(gate_send, zh=1)
    near_g = after(near_rows, gate_send)
    up_own, u_before, u_after = after((up_weight, u_before, u_after), gate_send)
    u_low = named(u_before[:cut], y=1)
    u_high = named(u_after[cut:], y=-1)
    u = (up_own, u_after, u_low, u_high, u_before)
    gate_near = over_cores(near_g, g)
    up_send = over_cores(far_rows, u).astype(BF)
    up_back = named(up_send, zh=1)
    near_u = after(near_rows, up_send)
    up_near = over_cores(near_u, u)
    gate = gate_near + gate_back.astype(F32)
    up = up_near + up_back.astype(F32)
    hidden = (jax.nn.silu(gate) * up).astype(BF)

    small = rank // 16
    at = lax.broadcasted_iota(jnp.int32, (rank, rank), 1)
    b = at // small
    src = ((b % 2 + zh) % 2 * 4 + b // 2 % 4) * 2 + (b // 8 + c) % 2
    src = src * small + at % small
    order = (lax.broadcasted_iota(jnp.int32, (rank, rank), 0) == src).astype(BF)
    test = jnp.dot(test_matrix, order, preferred_element_type=F32).astype(BF)

    part = jnp.dot(hidden, test, preferred_element_type=F32).astype(BF)
    part = lax.all_to_all(part.reshape(16, rows // 16, rank), ("x", "zl"), 0, 0, tiled=True)
    mine = jnp.sum(part.astype(F32), axis=0).astype(BF)
    copies = jnp.broadcast_to(mine[None], (16,) + mine.shape)
    projected = lax.all_to_all(copies, ("x", "zl"), 0, 0, tiled=True).reshape(rows, rank)

    update = lax.dot_general(
        projected, hidden, (((0,), (0,)), ((), ())), preferred_element_type=F32
    )
    half = rank // 2
    update = update[:half] + shift(update[half:].astype(BF), c=1).astype(F32)
    update = update.astype(BF).reshape(4, half // 4, width)
    update = lax.all_to_all(update, "y", 0, 0, tiled=True)
    update = jnp.sum(update.astype(F32), axis=0)
    summed = update[:small] + shift(update[small:].astype(BF), zh=1).astype(F32)
    return sketch_old + summed.T / (rows * 16)


def solution(mesh):
    fine = Mesh(mesh.devices.reshape(SIZES), AXES)
    dp = ("zh", "y", "c")
    tensor = ("x", "zl")
    in_specs = (P(dp, None), P(dp, tensor), P(dp, tensor), P(tensor, None), P(tensor, dp))
    return jax.shard_map(
        window, mesh=fine, in_specs=in_specs, out_specs=P(tensor, dp), check_vma=False
    )
```

```python
import jax
import jax.numpy as jnp
from jax import lax
from jax.experimental import pallas as pl
from jax.experimental.pallas import tpu as pltpu
from jax.sharding import Mesh, PartitionSpec as P


AXES = ("zh", "y", "c", "x", "zl")
SIZES = (2, 4, 2, 4, 4)
BF = jnp.bfloat16
F32 = jnp.float32


def shift(value, **moves):
    pairs = []
    total = 1
    for size in SIZES:
        total *= size
    for src in range(total):
        rest = src
        coords = []
        for size in reversed(SIZES):
            coords.append(rest % size)
            rest //= size
        coords = coords[::-1]
        dst = 0
        for name, size, at in zip(AXES, SIZES, coords):
            dst = dst * size + (at + moves.get(name, 0)) % size
        pairs.append((src, dst))
    return lax.ppermute(value, AXES, pairs)


def pick_columns(tokens, blocks, width):
    rows = tokens.shape[0]
    count = blocks.shape[0]

    def body(idx_ref, src_ref, dst_ref):
        dst_ref[0] = src_ref[...]

    return pl.pallas_call(
        body,
        grid_spec=pltpu.PrefetchScalarGridSpec(
            num_scalar_prefetch=1,
            grid=(count,),
            in_specs=[pl.BlockSpec((rows, width), lambda i, idx: (0, idx[i]))],
            out_specs=pl.BlockSpec((1, rows, width), lambda i, idx: (i, 0, 0)),
        ),
        out_shape=jax.ShapeDtypeStruct((count, rows, width), tokens.dtype),
        cost_estimate=pl.CostEstimate(
            flops=0, bytes_accessed=4 * count * rows * width, transcendentals=0
        ),
    )(blocks, tokens)


VMEM = pl.BlockSpec(memory_space=pltpu.VMEM)
SMEM = pl.BlockSpec(memory_space=pltpu.SMEM)


def product(lhs, slots, own_ref, other_ref):
    total = None
    for slot, parts in enumerate(slots):
        at = 0
        for part in parts:
            depth = part.shape[0]
            term = jnp.dot(lhs[slot, :, at : at + depth], part[...], preferred_element_type=F32)
            total = term if total is None else total + term
            at += depth
    rows = own_ref.shape[0]
    own_ref[...] = total[:rows]
    other_ref[...] = total[rows:].astype(BF)


def call_product(body, scalars, lhs, lhs_specs, weights, rows, extra):
    flat = [part for parts in weights for part in parts]
    blk, width = weights[0][0].shape
    counts = [len(parts) for parts in weights]

    def kernel(scalar_ref, *refs):
        lhs_refs = refs[: len(lhs)]
        rest = list(refs[len(lhs) :])
        slots = [[rest.pop(0) for _ in range(n)] for n in counts]
        own_ref, other_ref, stage = rest[:3]
        body(scalar_ref, lhs_refs, stage, *rest[3:])
        product(stage, slots, own_ref, other_ref)

    return pl.pallas_call(
        kernel,
        in_specs=[SMEM] + lhs_specs + [VMEM] * len(flat),
        out_specs=[VMEM, VMEM],
        out_shape=[
            jax.ShapeDtypeStruct((rows, width), F32),
            jax.ShapeDtypeStruct((rows, width), BF),
        ],
        scratch_shapes=[pltpu.VMEM((4, 2 * rows, blk), BF)] + extra,
        compiler_params=pltpu.CompilerParams(vmem_limit_bytes=32 << 20),
        cost_estimate=pl.CostEstimate(
            flops=16 * rows * blk * width, bytes_accessed=8 << 20, transcendentals=0
        ),
    )(scalars, *lhs, *flat)


def far_product(turn, pieces, weights):
    rows = pieces[0].shape[-2]

    def body(turn_ref, lhs_refs, stage):
        for half in range(2):
            for e in range(4):
                slot = (e + turn_ref[0]) % 4
                stage[slot, pl.ds(half * rows, rows), :] = lhs_refs[half * 4 + e][0]

    return call_product(body, turn, pieces, [VMEM] * 8, weights, rows, [])


def near_product(blocks, tokens, crossed, weights):
    rows = tokens.shape[0]
    blk = crossed.shape[-1]

    def body(blocks_ref, lhs_refs, stage, sems):
        tokens_ref, crossed_ref = lhs_refs
        copies = []
        for slot in range(4):
            at = pl.multiple_of(blocks_ref[slot] * blk, blk)
            copies.append(
                pltpu.make_async_copy(
                    tokens_ref.at[:, pl.ds(at, blk)], stage.at[slot, pl.ds(0, rows), :], sems.at[slot]
                )
            )
        for copy in copies:
            copy.start()
        for slot in range(4):
            stage[slot, pl.ds(rows, rows), :] = crossed_ref[slot]
        for copy in copies:
            copy.wait()

    specs = [pl.BlockSpec(memory_space=pl.ANY), VMEM]
    extra = [pltpu.SemaphoreType.DMA((4,))]
    return call_product(body, blocks, [tokens, crossed], specs, weights, rows, extra)


def arrange(where, test_matrix):
    rank = test_matrix.shape[1]
    small = rank // 16

    def kernel(where_ref, test_ref, out_ref):
        at = lax.broadcasted_iota(jnp.int32, (rank, rank), 1)
        b = at // small
        zh = (b % 2 + where_ref[0]) % 2
        y = (b // 2 + where_ref[1]) % 4
        c = (b // 8 + where_ref[2]) % 2
        src = ((zh * 4 + y) * 2 + c) * small + at % small
        order = lax.broadcasted_iota(jnp.int32, (rank, rank), 0) == src
        order = jnp.where(order, 1.0, 0.0).astype(BF)
        out_ref[...] = jnp.dot(test_ref[...], order, preferred_element_type=F32).astype(BF)

    return pl.pallas_call(
        kernel,
        in_specs=[SMEM, VMEM],
        out_specs=VMEM,
        out_shape=jax.ShapeDtypeStruct(test_matrix.shape, BF),
        cost_estimate=pl.CostEstimate(
            flops=2 * test_matrix.size * rank, bytes_accessed=2 << 20, transcendentals=0
        ),
    )(where, test_matrix)


def named(value, **moves):
    return shift(value, **moves)


def window(tokens, gate_weight, up_weight, test_matrix, sketch_old):
    zh, y, c, x = (lax.axis_index(name) for name in ("zh", "y", "c", "x"))
    rows = tokens.shape[0]
    blk, width = gate_weight.shape
    rank = test_matrix.shape[1]
    cut = blk // 2

    before = named(gate_weight, y=1)
    behind = named(gate_weight, y=-1)
    low = named(before[:cut], y=1)
    high = named(behind[cut:], y=-1)
    g = ((gate_weight,), (behind,), (low, high), (before,))
    up_low, up_high = up_weight[:cut], up_weight[cut:]
    before_low = named(up_low, y=1)
    behind_high = named(up_high, y=-1)
    low = named(before_low, y=1)
    high = named(behind_high, y=-1)
    before_high = named(up_high, y=1)
    behind_low = named(up_low, y=-1)
    u = ((up_weight,), (behind_low, behind_high), (low, high), (before_low, before_high))

    far = ((1 - zh) * 4 + x) * 2
    cross = pick_columns(tokens, jnp.stack([far + 1 - c]).astype(jnp.int32), blk)
    keep = pick_columns(tokens, jnp.stack([far + c]).astype(jnp.int32), blk)
    cross = named(named(cross, zh=1), c=1)
    keep = named(keep, zh=1)
    far_rows = []
    for piece in (keep, cross):
        far_rows += [piece, named(piece, x=-1), named(piece, x=2), named(piece, x=1)]
    turn = ((x - y) % 4).astype(jnp.int32).reshape(1)

    where = jnp.stack([zh, y, c]).astype(jnp.int32)
    test = arrange(where, test_matrix)

    near = [(zh * 4 + (y + s) % 4) * 2 for s in range(4)]
    c_send = pick_columns(tokens, jnp.stack([n + 1 - c for n in near]).astype(jnp.int32), blk)
    crossed = named(c_send, c=1)
    near_blocks = jnp.stack([n + c for n in near]).astype(jnp.int32)

    def over_cores(own, other):
        return own + named(other, c=1).astype(F32)

    gate_send = over_cores(*far_product(turn, far_rows, g)).astype(BF)
    gate_back = named(gate_send, zh=1)
    up_send = over_cores(*far_product(turn, far_rows, u)).astype(BF)
    up_back = named(up_send, zh=1)
    gate = over_cores(*near_product(near_blocks, tokens, crossed, g))
    up = over_cores(*near_product(near_blocks, tokens, crossed, u))
    gate = gate + gate_back.astype(F32)
    up = up + up_back.astype(F32)
    hidden = (jax.nn.silu(gate) * up).astype(BF)

    small = rank // 16
    part = jnp.dot(hidden, test, preferred_element_type=F32).astype(BF)
    part = lax.all_to_all(part.reshape(16, rows // 16, rank), ("x", "zl"), 0, 0, tiled=True)
    mine = jnp.sum(part.astype(F32), axis=0).astype(BF)
    copies = jnp.broadcast_to(mine[None], (16,) + mine.shape)
    projected = lax.all_to_all(copies, ("x", "zl"), 0, 0, tiled=True).reshape(rows, rank)

    update = lax.dot_general(
        projected, hidden, (((0,), (0,)), ((), ())), preferred_element_type=F32
    )
    half = rank // 2
    update = update[:half] + shift(update[half:].astype(BF), c=1).astype(F32)
    update = update.reshape(4, half // 4, width)
    sends = update[1:].astype(BF)
    gots = [shift(sends[k - 1], y=k) for k in (1, 3, 2)]
    update = update[0] + sum(got.astype(F32) for got in gots)
    summed = update[:small] + shift(update[small:].astype(BF), zh=1).astype(F32)
    return sketch_old + summed.T / (rows * 16)


def solution(mesh):
    fine = Mesh(mesh.devices.reshape(SIZES), AXES)
    dp = ("zh", "y", "c")
    tensor = ("x", "zl")
    in_specs = (P(dp, None), P(dp, tensor), P(dp, tensor), P(tensor, None), P(tensor, dp))
    return jax.shard_map(
        window, mesh=fine, in_specs=in_specs, out_specs=P(tensor, dp), check_vma=False
    )
```
